32 devices in a mesh: outer: 4 (over y, x), inner: 8 (over z, core).
Axes of the slice: x: 2, y: 2, z: 4, core: 2. Of those that a mesh axis runs over, the one named last changes fastest.
Arguments:
- queries: bfloat16 [8192, 1024], P(('outer', 'inner')), may hold values from -480 to 480
- keys: bfloat16 [8192, 512], P(('outer', 'inner')), may hold values from -8 to 8
- values: bfloat16 [8192, 512], P(('outer', 'inner')), may hold values from -4 to 4
- residual: bfloat16 [8192, 1024], P(('outer', 'inner')), may hold values from -5 to 5
- norm_gain: float32 [1024], replicated, may hold values from 0.1 to 1.9
- w_gate: bfloat16 [8, 1024, 512], P('inner'), may hold values from -0.1875 to 0.1875
- w_up: bfloat16 [8, 1024, 512], P('inner'), may hold values from -0.1875 to 0.1875
- w_down: bfloat16 [8, 512, 1024], P('inner'), may hold values from -0.25 to 0.25
- routes: int32 [8192, 2], P(('outer', 'inner')), may hold values from 0 to 7, all different within a row; in each aligned block of 256 rows (0 to 255, 256 to 511, ...) at most 128 rows name the same one
- gates: float32 [8192, 2], P(('outer', 'inner')), may hold values from 0.2 to 1
Outputs:
- layer_out: bfloat16 [8192, 1024], P(('outer', 'inner'))
The draws below stay inside these ranges and needn't reach their ends.
Inputs may be any that keep to these rules, and one draw needn't show every extreme that they name: `routes`: A patch's two experts differ. Within one block of 256 patches no expert is picked more than 128 times, and in some block one expert is picked exactly 128 times.
All inputs are finite; a program needn't handle non-finite values.
Results may differ from the reference program's by a relative error of at most 0.0085.
Values may be sent and summed in bfloat16 or wider, within the bound.
A program may use at most 64 MiB of HBM per device.

```python
import math
import jax
import jax.numpy as jnp
import numpy as np
from jax import lax

D = 1024
QH = 8
KVH = 4
DH = 128
FF = 512
BACK = 3
TOK_DEV = 256
EXPERTS = 8
CAP = 128
TOKENS = 8192


def paired_draw(key):
    folded = jax.random.fold_in(key, 4471)
    key_q, key_k = jax.random.split(folded)
    query_draw = 1.7 * jax.random.truncated_normal(key_q, -4.5, 4.5, (TOKENS, QH * DH), jnp.float32)
    key_draw = 1.7 * jax.random.truncated_normal(key_k, -4.5, 4.5, (TOKENS, KVH * DH), jnp.float32)
    return (query_draw, key_draw)


def draw_queries(key, part):
    return paired_draw(key)[0].astype(jnp.bfloat16)


def draw_keys(key, part):
    return paired_draw(key)[1].astype(jnp.bfloat16)


def levels(stream_key, shape, shards, least, high):
    def one(axis_at, shards_of):
        heights = jax.random.uniform(jax.random.fold_in(jax.random.fold_in(stream_key, 6), axis_at), (shards_of,), jnp.float32, least / len(shards), high / len(shards))
        return jnp.repeat(jnp.exp(heights), shape[axis_at] // shards_of).reshape((-1,) + (1,) * (len(shape) - axis_at - 1))

    gain = one(*shards[0])
    for cut in shards[1:]:
        gain = gain * one(*cut)
    return gain


def assign_block(key, own, number, rows, count, top, reach, slope):
    sequence = jax.random.permutation(key, count)
    heavy_load, usual = load_shares(count, rows * top, reach, slope, True), load_shares(count, rows * top, reach, slope, False)
    places = jnp.arange(count)

    def named(tallies, turn):
        used = int((tallies > 0).sum())
        fixed = max(1, used // 4)
        shifted = fixed + (places - fixed + turn * (used - fixed)) % max(1, count - fixed)
        return jnp.zeros((count,), jnp.int32).at[sequence[jnp.where(places < fixed, places, shifted)]].set(jnp.asarray(tallies, jnp.int32))

    tallies = jnp.where(number % 4 == 0, named(heavy_load, number // 4), named(usual, number - number // 4 - 1))
    mixed = jax.random.permutation(jax.random.fold_in(own, 3), count)
    donor, taker = mixed[0:count // 2 * 2:2], mixed[1:count // 2 * 2:2]
    room = jnp.minimum(tallies[donor] - 1, reach - tallies[taker]) // 2
    room = jnp.where((donor == sequence[0]) | (taker == sequence[0]) | (tallies[taker] == 0), 0, jnp.maximum(room, 0))
    shifted = jax.random.randint(jax.random.fold_in(own, 4), (count // 2,), 0, 1 << 20) % (room + 1)
    tallies = tallies.at[donor].add(-shifted).at[taker].add(shifted)
    labels = jnp.searchsorted(jnp.cumsum(tallies), jnp.arange(rows * top), side="right").astype(jnp.int32)
    table = labels.reshape(top, rows).T
    table = table[jax.random.permutation(jax.random.fold_in(own, 1), rows)]
    turn = jax.random.randint(jax.random.fold_in(own, 2), (rows, 1), 0, top)
    return jnp.take_along_axis(table, (jnp.arange(top)[None, :] + turn) % top, axis=1)


def load_shares(amount, total, limit, lean, full):
    portions = [(1 << 20) // math.isqrt(rank ** lean) + 1 for rank in range(1, amount + 1)]
    largest = limit if full else min(limit, max(-(-total // amount), total * portions[0] // sum(portions)))
    least = 1 if total - largest >= amount - 1 else 0
    counts, surplus = [largest] + [least] * (amount - 1), total - largest - least * (amount - 1)
    while surplus > 0:
        candidates = [i for i in range(1, amount) if counts[i] < largest] or [i for i in range(1, amount) if counts[i] < limit]
        pool, left = sum([portions[i] for i in candidates]), surplus
        for i in candidates:
            extra = min(limit - counts[i], max(1, left * portions[i] // pool), surplus)
            counts[i] = counts[i] + extra
            surplus = surplus - extra
    return np.array(counts)


def gaussian(own_key, dims, width, limit, pieces=(), kind=jnp.bfloat16):
    factor_of = levels(own_key, dims, pieces, -0.22, 0.18) if pieces else 1.0
    entries = jax.random.normal(own_key, dims, jnp.float32) * width * factor_of
    return jnp.minimum(jnp.maximum(entries, -limit), limit).astype(kind)


def setup_inputs(seed: int = 0) -> dict:
    splits = jax.random.split(jax.random.key(seed), 11)
    queries = draw_queries(jax.random.fold_in(splits[10], 71), 0)
    keys = draw_keys(jax.random.fold_in(splits[10], 71), 0)
    values = gaussian(splits[2], (TOKENS, KVH * DH), 1.0, 4.0, ((0, 32),))
    residual = gaussian(splits[3], (TOKENS, D), 1.0, 5.0, ((0, 32),))
    norm_gain = jnp.clip(1.0 + 0.18 * jax.random.normal(splits[4], (D,), jnp.float32), 0.1, 1.9)
    w_gate = gaussian(splits[5], (EXPERTS, D, FF), D ** -0.5, 0.1875, ((0, 8),))
    w_up = gaussian(splits[6], (EXPERTS, D, FF), D ** -0.5, 0.1875, ((0, 8),))
    w_down = gaussian(splits[7], (EXPERTS, FF, D), FF ** -0.5, 0.25, ((0, 8),))
    routes_keys = jax.random.split(jax.random.fold_in(splits[8], 1), TOKENS // TOK_DEV)
    routes_turns = jax.random.permutation(jax.random.fold_in(splits[8], 3), TOKENS // TOK_DEV)
    routes = jax.vmap(lambda own, number: assign_block(jax.random.fold_in(splits[8], 2), own, number, TOK_DEV, EXPERTS, 2, CAP, 2))(routes_keys, routes_turns).reshape((TOKENS, 2))
    gates = jnp.clip(0.2 + 0.8 * jax.random.uniform(splits[9], (TOKENS, 2), jnp.float32) ** levels(splits[9], (TOKENS, 2), ((0, 32),), -0.2, 0.2), 0.2, 1.0)
    return dict(queries=queries, keys=keys, values=values, residual=residual, norm_gain=norm_gain, w_gate=w_gate, w_up=w_up, w_down=w_down, routes=routes, gates=gates)


def feed_forward(rows, gate_matrix, up_matrix, down_matrix):
    gate_part = jnp.dot(rows, gate_matrix, preferred_element_type=jnp.float32)
    up_part = jnp.dot(rows, up_matrix, preferred_element_type=jnp.float32)
    inner_act = (jax.nn.silu(gate_part) * up_part).astype(jnp.bfloat16)
    return jnp.dot(inner_act, down_matrix, preferred_element_type=jnp.float32).astype(jnp.bfloat16)

def reference(queries, keys, values, residual, norm_gain, w_gate, w_up, w_down, routes, gates):
    groups = QH // KVH
    nblocks = TOKENS // TOK_DEV
    pad_rows = BACK * TOK_DEV
    window_rows = (BACK + 1) * TOK_DEV
    keys_pad = jnp.concatenate([jnp.zeros((pad_rows, KVH * DH), keys.dtype), keys], 0)
    values_pad = jnp.concatenate([jnp.zeros((pad_rows, KVH * DH), values.dtype), values], 0)
    scale = 1.0 / math.sqrt(DH)

    def attend(block_id):
        start = (block_id * TOK_DEV).astype(jnp.int32)
        query_block = lax.dynamic_slice_in_dim(queries, start, TOK_DEV, 0).astype(jnp.float32).reshape(TOK_DEV, KVH, groups, DH)
        key_block = lax.dynamic_slice_in_dim(keys_pad, start, window_rows, 0).astype(jnp.float32).reshape(window_rows, KVH, DH)
        value_block = lax.dynamic_slice_in_dim(values_pad, start, window_rows, 0).astype(jnp.float32).reshape(window_rows, KVH, DH)
        scores = jnp.einsum('tkgd,skd->kgts', query_block, key_block) * scale
        query_pos = start + jnp.arange(TOK_DEV, dtype=jnp.int32)
        key_pos = start - pad_rows + jnp.arange(window_rows, dtype=jnp.int32)
        allowed = (key_pos[None, :] >= 0) & (key_pos[None, :] <= query_pos[:, None])
        scores = jnp.where(allowed, scores, -jnp.inf)
        highest = lax.optimization_barrier(jnp.max(scores, -1, keepdims=True))
        expd = jnp.exp(scores - highest)
        weights = (expd / lax.optimization_barrier(jnp.sum(expd, -1, keepdims=True))).astype(jnp.bfloat16)
        mixed = jnp.einsum('kgts,skd->tkgd', weights.astype(jnp.float32), value_block)
        return mixed.astype(jnp.bfloat16).reshape(TOK_DEV, QH * DH)
    attended = lax.map(attend, jnp.arange(nblocks, dtype=jnp.int32)).reshape(TOKENS, QH * DH)
    stream = residual.astype(jnp.float32) + attended.astype(jnp.float32)
    mean_sq = lax.optimization_barrier(jnp.mean(stream * stream, -1, keepdims=True))
    normed = (stream * lax.rsqrt(mean_sq + 1e-06) * norm_gain).astype(jnp.bfloat16)
    capacity = 4 * TOK_DEV // EXPERTS
    per_expert = nblocks * capacity
    picks = routes.reshape(nblocks, 2 * TOK_DEV).astype(jnp.int32)
    one_hot = (picks[:, :, None] == jnp.arange(EXPERTS, dtype=jnp.int32)[None, None, :]).astype(jnp.int32)
    order_rank = lax.optimization_barrier(jnp.sum((jnp.cumsum(one_hot, 1) - 1) * one_hot, -1)).astype(jnp.int32)
    slot_index = (picks * per_expert + jnp.arange(nblocks, dtype=jnp.int32)[:, None] * capacity + order_rank).reshape(-1).astype(jnp.int32)
    token_of_pick = (jnp.arange(2 * TOKENS, dtype=jnp.int32) // 2).astype(jnp.int32)
    table = jnp.full((EXPERTS * per_expert,), TOKENS, jnp.int32).at[slot_index].set(token_of_pick)
    padded = jnp.concatenate([normed, jnp.zeros((1, D), normed.dtype)], 0)

    def run_expert(expert_id):
        rows = padded[lax.dynamic_slice_in_dim(table, (expert_id * per_expert).astype(jnp.int32), per_expert, 0)]
        return feed_forward(rows, w_gate[expert_id], w_up[expert_id], w_down[expert_id])
    expert_out = lax.map(run_expert, jnp.arange(EXPERTS, dtype=jnp.int32)).reshape(EXPERTS * per_expert, D)
    picked = expert_out[slot_index].astype(jnp.float32).reshape(TOKENS, 2, D)
    mixture = lax.optimization_barrier(jnp.sum(gates[:, :, None] * picked, 1))
    return (stream + mixture).astype(jnp.bfloat16)
```

```python
import functools
import math

import jax
import jax.numpy as jnp
from jax import lax
from jax.experimental import pallas as pl
from jax.experimental.pallas import tpu as pltpu
from jax.sharding import PartitionSpec as P

D = 1024
QH = 8
KVH = 4
DH = 128
BACK = 3


def shifted(value, axis, steps):
    count = lax.axis_size(axis)
    first, last = (max(0, -steps), min(count, count - steps))
    return lax.ppermute(value, axis, [(source, source + steps) for source in range(first, last)])


MESH = pl.DeviceIdType.MESH
CHUNKS = 4


def expert_kernel(
    lanes, normed_ref, stream_ref, shares_ref, gate_ref, up_ref, down_ref, out_ref,
    rows, parts, mate_in, line_in, share_in,
    share_send, share_recv, row_send, row_recv, mate_send, mate_recv,
    give_send, give_recv, sum_send, sum_recv,
):
    inner = lax.axis_index("inner")
    spots = lanes // 2
    spot, core = inner // 2, inner % 2
    mate = 2 * spot + (1 - core)
    tok_rows = normed_ref.shape[0]
    piece = tok_rows // CHUNKS

    def at_piece(k):
        return pl.ds(k * piece, piece)

    def remote(src, dst, send, recv, to):
        return pltpu.make_async_remote_copy(
            src_ref=src, dst_ref=dst, send_sem=send, recv_sem=recv,
            device_id={"inner": to}, device_id_type=MESH,
        )

    above, below = inner + 2, inner - 2
    has_above, has_below = spot < spots - 1, spot > 0

    barrier = pltpu.get_barrier_semaphore()

    @pl.loop(1, lanes)
    def _(step):
        pl.semaphore_signal(
            barrier, inc=1, device_id={"inner": lax.rem(inner + step, lanes)}, device_id_type=MESH
        )

    pl.semaphore_wait(barrier, lanes - 1)

    def row_copy(src, where, sem, k, to):
        return remote(src, rows.at[where, core, at_piece(k)], row_send.at[sem, k], row_recv.at[where, k], to)

    def mate_copy(src, where, k):
        return remote(src, rows.at[where, core, at_piece(k)], mate_send.at[where, k], mate_recv.at[where, k], mate)

    def give_copy(where):
        return remote(parts.at[where, 1 - core], mate_in.at[where], give_send.at[where], give_recv.at[where], mate)

    def sum_copy(where, slot, k, to):
        return remote(
            parts.at[where, core, at_piece(k)], line_in.at[slot, at_piece(k)],
            sum_send.at[where, k], sum_recv.at[slot, k], to,
        )

    for k in range(CHUNKS):
        own = normed_ref.at[at_piece(k)]

        @pl.when(has_above)
        def _():
            row_copy(own, spot, spot, k, above).start()

        @pl.when(has_below)
        def _():
            row_copy(own, spot, spots, k, below).start()

        mate_copy(own, spot, k).start()

    def share_copy(to):
        return remote(shares_ref.at[to], share_in.at[inner], share_send.at[to], share_recv.at[inner], to)

    @pl.loop(1, lanes)
    def _(step):
        share_copy(lax.rem(inner + step, lanes)).start()

    share_in[inner] = shares_ref[inner]
    rows[spot, core] = normed_ref[...]

    @pl.loop(1, lanes)
    def _(step):
        source = lax.rem(inner + step, lanes)
        remote(
            shares_ref.at[source], share_in.at[source], share_send.at[source], share_recv.at[source], source
        ).wait_recv()

    def experts_on(where):
        @pl.loop(0, 2)
        def _(side):
            block = rows[where, side]
            gate_part = jnp.dot(block, gate_ref[0], preferred_element_type=jnp.float32)
            up_part = jnp.dot(block, up_ref[0], preferred_element_type=jnp.float32)
            act = (gate_part / (1.0 + jnp.exp(-gate_part)) * up_part).astype(jnp.bfloat16)
            result = jnp.dot(act, down_ref[0], preferred_element_type=jnp.float32)
            share = share_in[2 * where + side]
            row_id = lax.broadcasted_iota(jnp.int32, (tok_rows, tok_rows), 0)
            col_id = lax.broadcasted_iota(jnp.int32, (tok_rows, tok_rows), 1)
            column = jnp.sum(
                jnp.where(row_id == col_id, jnp.broadcast_to(share, (tok_rows, tok_rows)), 0.0),
                axis=1, keepdims=True,
            )
            result = result.astype(jnp.bfloat16).astype(jnp.float32)
            parts[where, side] = (result * column).astype(jnp.bfloat16)

        give_copy(where).start()

    def take_rows(where, onward, to):
        for k in range(CHUNKS):
            here = rows.at[where, core, at_piece(k)]
            row_copy(here, where, where, k, to).wait_recv()

            @pl.when(onward)
            def _():
                row_copy(here, where, where, k, to).start()

            mate_copy(here, where, k).start()
        for k in range(CHUNKS):
            mate_copy(rows.at[where, core, at_piece(k)], where, k).wait_recv()

    def pass_sum(where, slot_to, more, to):
        give_copy(where).wait_recv()
        for k in range(CHUNKS):
            at = at_piece(k)

            @pl.when(more)
            def _():
                sum_copy(where, where, k, to).wait_recv()
                parts[where, core, at] = (
                    parts[where, core, at].astype(jnp.float32)
                    + mate_in[where, at].astype(jnp.float32)
                    + line_in[where, at].astype(jnp.float32)
                ).astype(jnp.bfloat16)

            @pl.when(jnp.logical_not(more))
            def _():
                parts[where, core, at] = (
                    parts[where, core, at].astype(jnp.float32) + mate_in[where, at].astype(jnp.float32)
                ).astype(jnp.bfloat16)

            sum_copy(where, slot_to, k, to).start()

    for k in range(CHUNKS):
        mate_copy(normed_ref.at[at_piece(k)], spot, k).wait_recv()
    experts_on(spot)

    @pl.loop(1, max(2 * spots - 2, 1))
    def _(time):
        low, high = spot - time, spot + time

        @pl.when(low >= 0)
        def _():
            take_rows(low, has_above, jnp.minimum(above, lanes - 2 + core))

        @pl.when(high < spots)
        def _():
            take_rows(high, has_below, jnp.maximum(below, core))

        @pl.when(low >= 0)
        def _():
            experts_on(low)

        @pl.when(high < spots)
        def _():
            experts_on(high)

        down = 2 * spots - 2 - spot - time

        @pl.when((down >= 0) & (down < spot))
        def _():
            pass_sum(down, jnp.where(down == spot - 1, down, down), has_above, below)

        up = time - spot

        @pl.when((up > spot) & (up < spots))
        def _():
            pass_sum(up, jnp.where(up == spot + 1, spots, up), has_below, above)

    give_copy(spot).wait_recv()
    for k in range(CHUNKS):
        at = at_piece(k)
        out = parts[spot, core, at].astype(jnp.float32) + mate_in[spot, at].astype(jnp.float32)
        stash = stream_ref[at, :] + out
        out_ref[at, :] = stash.astype(jnp.bfloat16)

        @pl.when(has_above & has_below)
        def _():
            sum_copy(spot, spot, k, above).wait_recv()
            sum_copy(spot, spots, k, above).wait_recv()
            out_ref[at, :] = (
                stash + line_in[spot, at].astype(jnp.float32) + line_in[spots, at].astype(jnp.float32)
            ).astype(jnp.bfloat16)

        @pl.when(has_above & jnp.logical_not(has_below))
        def _():
            sum_copy(spot, spot, k, above).wait_recv()
            out_ref[at, :] = (stash + line_in[spot, at].astype(jnp.float32)).astype(jnp.bfloat16)

        @pl.when(has_below & jnp.logical_not(has_above))
        def _():
            sum_copy(spot, spots, k, below).wait_recv()
            out_ref[at, :] = (stash + line_in[spots, at].astype(jnp.float32)).astype(jnp.bfloat16)

    @pl.loop(1, lanes)
    def _(step):
        share_copy(lax.rem(inner + step, lanes)).wait_send()

    for k in range(CHUNKS):
        own = normed_ref.at[at_piece(k)]

        @pl.when(has_above)
        def _():
            row_copy(own, spot, spot, k, above).wait_send()

        @pl.when(has_below)
        def _():
            row_copy(own, spot, spots, k, below).wait_send()

        mate_copy(own, spot, k).wait_send()

    @pl.loop(0, spots)
    def _(where):
        give_copy(where).wait_send()

        @pl.when(where != spot)
        def _():
            to = jnp.where(where < spot, jnp.minimum(above, lanes - 2 + core), jnp.maximum(below, core))
            back = jnp.where(where < spot, inner - 2, inner + 2)
            onward = ((where < spot) & has_above) | ((where > spot) & has_below)
            for k in range(CHUNKS):
                here = rows.at[where, core, at_piece(k)]
                mate_copy(here, where, k).wait_send()
                sum_copy(where, where, k, back).wait_send()

                @pl.when(onward)
                def _():
                    row_copy(here, where, where, k, to).wait_send()


def expert_layer(lanes, normed, stream, shares, w_gate, w_up, w_down):
    tok_rows, width = normed.shape
    spots = lanes // 2
    vmem = pl.BlockSpec(memory_space=pltpu.VMEM)
    dma = pltpu.SemaphoreType.DMA
    return pl.pallas_call(
        functools.partial(expert_kernel, lanes),
        out_shape=jax.ShapeDtypeStruct((tok_rows, width), jnp.bfloat16),
        in_specs=[vmem] * 6,
        out_specs=vmem,
        scratch_shapes=[
            pltpu.VMEM((spots, 2, tok_rows, width), jnp.bfloat16),
            pltpu.VMEM((spots, 2, tok_rows, width), jnp.bfloat16),
            pltpu.VMEM((spots, tok_rows, width), jnp.bfloat16),
            pltpu.VMEM((spots + 1, tok_rows, width), jnp.bfloat16),
            pltpu.VMEM((lanes, 1, tok_rows), jnp.float32),
            dma((lanes,)), dma((lanes,)),
            dma((spots + 1, CHUNKS)), dma((spots, CHUNKS)),
            dma((spots, CHUNKS)), dma((spots, CHUNKS)),
            dma((spots,)), dma((spots,)),
            dma((spots, CHUNKS)), dma((spots + 1, CHUNKS)),
        ],
        compiler_params=pltpu.CompilerParams(
            collective_id=0, has_side_effects=True, vmem_limit_bytes=60 * 1024 * 1024
        ),
    )(normed, stream, shares, w_gate, w_up, w_down)


def local(queries, keys, values, residual, norm_gain, w_gate, w_up, w_down, routes, gates):
    tok_rows = queries.shape[0]
    groups = QH // KVH
    device_index = lax.axis_index(("outer", "inner"))
    current = (keys, values)
    earlier = []
    for step_index in range(BACK):
        current = shifted((current[0], current[1]), ("outer", "inner"), 1)
        earlier = [current] + earlier
    key_window = jnp.concatenate([block_pair[0] for block_pair in earlier] + [keys], 0)
    value_window = jnp.concatenate([block_pair[1] for block_pair in earlier] + [values], 0)
    window_rows = key_window.shape[0]
    query_heads = queries.reshape(tok_rows, KVH, groups, DH)
    key_heads = key_window.reshape(window_rows, KVH, DH)
    value_heads = value_window.reshape(window_rows, KVH, DH)
    scores = jnp.einsum(
        "tkgd,skd->kgts", query_heads, key_heads, preferred_element_type=jnp.float32
    ) * (1.0 / math.sqrt(DH))
    query_pos = device_index * tok_rows + jnp.arange(tok_rows, dtype=jnp.int32)
    key_pos = (device_index - BACK) * tok_rows + jnp.arange(window_rows, dtype=jnp.int32)
    allowed = (key_pos[None, :] >= 0) & (key_pos[None, :] <= query_pos[:, None])
    scores = jnp.where(allowed, scores, -jnp.inf)
    highest = jnp.max(scores, -1, keepdims=True)
    expd = jnp.exp(scores - highest)
    weights = (expd / jnp.sum(expd, -1, keepdims=True)).astype(jnp.bfloat16)
    mixed = jnp.einsum("kgts,skd->tkgd", weights, value_heads, preferred_element_type=jnp.float32)
    attended = mixed.astype(jnp.bfloat16).reshape(tok_rows, QH * DH)
    stream = residual.astype(jnp.float32) + attended.astype(jnp.float32)
    mean_sq = jnp.mean(stream * stream, -1, keepdims=True)
    normed = (stream * lax.rsqrt(mean_sq + 1e-06) * norm_gain).astype(jnp.bfloat16)
    owners = lax.axis_size("inner")
    named = routes.T[:, None, :] == jnp.arange(owners, dtype=jnp.int32)[None, :, None]
    shares = jnp.sum(jnp.where(named, gates.T[:, None, :], 0.0), 0)[:, None, :]
    return expert_layer(owners, normed, stream, shares, w_gate, w_up, w_down)


def solution(mesh):
    return jax.shard_map(
        local,
        mesh=mesh,
        in_specs=(
            P(("outer", "inner"), None),
            P(("outer", "inner"), None),
            P(("outer", "inner"), None),
            P(("outer", "inner"), None),
            P(),
            P("inner", None, None),
            P("inner", None, None),
            P("inner", None, None),
            P(("outer", "inner"), None),
            P(("outer", "inner"), None),
        ),
        out_specs=P(("outer", "inner"), None),
        check_vma=False,
    )
```

```python
import functools
import math

import jax
import jax.numpy as jnp
from jax import lax
from jax.experimental import pallas as pl
from jax.experimental.pallas import tpu as pltpu
from jax.sharding import PartitionSpec as P

D = 1024
QH = 8
KVH = 4
DH = 128
BACK = 3


MESH = pl.DeviceIdType.MESH
CHUNKS = 4


def expert_kernel(
    lanes, total, query_ref, key_ref, value_ref, residual_ref, gain_ref, route_ref, pick_ref,
    gate_ref, up_ref, down_ref, out_ref,
    key_halo, value_halo, top, mass, stream, shares_ref, halo_send, halo_recv, rows, parts, mate_in, line_in, share_in,
    share_send, share_recv, row_send, row_recv, mate_send, mate_recv,
    give_send, give_recv, sum_send, sum_recv,
):
    inner = lax.axis_index("inner")
    spots = lanes // 2
    spot, core = inner // 2, inner % 2
    mate = 2 * spot + (1 - core)
    tok_rows = query_ref.shape[0]
    groups = QH // KVH
    place = lax.axis_index("outer") * lanes + inner
    piece = tok_rows // CHUNKS

    def at_piece(k):
        return pl.ds(k * piece, piece)

    def remote(src, dst, send, recv, to):
        return pltpu.make_async_remote_copy(
            src_ref=src, dst_ref=dst, send_sem=send, recv_sem=recv,
            device_id={"inner": to}, device_id_type=MESH,
        )

    above, below = inner + 2, inner - 2
    has_above, has_below = spot < spots - 1, spot > 0

    barrier = pltpu.get_barrier_semaphore()

    @pl.loop(1, lanes)
    def _(step):
        pl.semaphore_signal(
            barrier, inc=1, device_id={"inner": lax.rem(inner + step, lanes)}, device_id_type=MESH
        )

    def whole_id(to):
        return {"outer": to // lanes, "inner": lax.rem(to, lanes)}

    expected = lanes - 1
    for shift in (-2, -1, 1, 2):
        other = place + shift
        reaches = (other >= 0) & (other < total)

        @pl.when(reaches)
        def _():
            pl.semaphore_signal(barrier, inc=1, device_id=whole_id(other), device_id_type=MESH)

        expected = expected + reaches.astype(jnp.int32)

    @pl.loop(0, lanes)
    def _(expert):
        chosen = jnp.where(route_ref[...] == expert, pick_ref[...], 0.0)
        shares_ref[expert] = jnp.sum(chosen, axis=0, keepdims=True)

    pl.semaphore_wait(barrier, expected)

    even = core == 0
    halos = ((key_ref, key_halo), (value_ref, value_halo))

    def halo_copy(kind, held, ahead, lane):
        own_ref, halo = halos[kind]
        src = own_ref if held == 0 else halo.at[held - 1]
        return pltpu.make_async_remote_copy(
            src_ref=src, dst_ref=halo.at[held + ahead - 1],
            send_sem=halo_send.at[kind, lane], recv_sem=halo_recv.at[kind, held + ahead - 1],
            device_id=whole_id(jnp.minimum(place + ahead, total - 1)), device_id_type=MESH,
        )

    goes_one = place + 1 < total
    goes_two = even & (place + 2 < total)
    plan = (
        (0, 1, goes_one),
        (0, 2, goes_two),
        (1, 1, even & (place >= 1)),
        (1, 2, goes_two & (place >= 1)),
        (2, 1, even & (place >= 2)),
    )

    def halo_start(kind, lane):
        held, ahead, active = plan[lane]

        @pl.when(active)
        def _():
            halo_copy(kind, held, ahead, lane).start()

    def halo_wait(kind, held):
        own_ref, halo = halos[kind]

        @pl.when(place >= held)
        def _():
            pltpu.make_async_remote_copy(
                src_ref=own_ref, dst_ref=halo.at[held - 1],
                send_sem=halo_send.at[kind, 0], recv_sem=halo_recv.at[kind, held - 1],
                device_id=whole_id(jnp.maximum(place - 1, 0)), device_id_type=MESH,
            ).wait_recv()

    for lane in (1, 0):
        halo_start(0, lane)
    for lane in (1, 0):
        halo_start(1, lane)

    def attend(held):
        @pl.loop(0, KVH)
        def _(head):
            wide = pl.ds(pl.multiple_of(head * groups * DH, groups * DH), groups * DH)
            narrow = pl.ds(pl.multiple_of(head * DH, DH), DH)
            asked = query_ref[:, wide]
            if held == 0:
                keys, vals = key_ref[:, narrow], value_ref[:, narrow]
            else:
                keys, vals = key_halo[held - 1, :, narrow], value_halo[held - 1, :, narrow]
            mixed = []
            for group in range(groups):
                scores = lax.dot_general(
                    asked[:, group * DH : (group + 1) * DH], keys, (((1,), (1,)), ((), ())),
                    preferred_element_type=jnp.float32,
                ) * (1.0 / math.sqrt(DH))
                if held == 0:
                    row_id = lax.broadcasted_iota(jnp.int32, scores.shape, 0)
                    col_id = lax.broadcasted_iota(jnp.int32, scores.shape, 1)
                    scores = jnp.where(col_id <= row_id, scores, -jnp.inf)
                highest = jnp.max(scores, -1, keepdims=True)
                slot = head * groups + group
                if held:
                    highest = jnp.maximum(top[slot], highest)
                expd = jnp.exp(scores - highest)
                summed = jnp.sum(expd, -1, keepdims=True)
                part = jnp.dot(expd.astype(jnp.bfloat16), vals, preferred_element_type=jnp.float32)
                if held:
                    keep = jnp.exp(top[slot] - highest)
                    summed = summed + mass[slot] * keep
                    at = pl.ds(pl.multiple_of(slot * DH, DH), DH)
                    part = part + stream[:, at] * keep
                top[slot] = highest
                mass[slot] = summed
                mixed.append(part)
            stream[:, wide] = jnp.concatenate(mixed, 1)

    attend(0)
    for kind in range(2):
        halo_wait(kind, 1)
        halo_start(kind, 3)
        halo_start(kind, 2)
        halo_wait(kind, 2)
        halo_start(kind, 4)
    for held in range(1, BACK + 1):
        if held == BACK:
            halo_wait(0, held)
            halo_wait(1, held)

        @pl.when(place >= held)
        def _():
            attend(held)

    @pl.loop(0, QH)
    def _(slot):
        at = pl.ds(pl.multiple_of(slot * DH, DH), DH)
        attended = (stream[:, at] / mass[slot]).astype(jnp.bfloat16).astype(jnp.float32)
        stream[:, at] = residual_ref[:, at].astype(jnp.float32) + attended

    for k in range(CHUNKS):
        at = pl.ds(k * piece, piece)
        kept = stream[at, :]
        mean_sq = jnp.mean(kept * kept, -1, keepdims=True)
        rows[spot, core, at] = (kept * lax.rsqrt(mean_sq + 1e-06) * gain_ref[...]).astype(jnp.bfloat16)

    def row_copy(src, where, sem, k, to):
        return remote(src, rows.at[where, core, at_piece(k)], row_send.at[sem, k], row_recv.at[where, k], to)

    def mate_copy(src, where, k):
        return remote(src, rows.at[where, core, at_piece(k)], mate_send.at[where, k], mate_recv.at[where, k], mate)

    def give_copy(where):
        return remote(parts.at[where, 1 - core], mate_in.at[where], give_send.at[where], give_recv.at[where], mate)

    def sum_copy(where, slot, k, to):
        return remote(
            parts.at[where, core, at_piece(k)], line_in.at[slot, at_piece(k)],
            sum_send.at[where, k], sum_recv.at[slot, k], to,
        )

    for k in range(CHUNKS):
        own = rows.at[spot, core, at_piece(k)]

        @pl.when(has_above)
        def _():
            row_copy(own, spot, spot, k, above).start()

        @pl.when(has_below)
        def _():
            row_copy(own, spot, spots, k, below).start()

        mate_copy(own, spot, k).start()

    def share_copy(to):
        return remote(shares_ref.at[to], share_in.at[inner], share_send.at[to], share_recv.at[inner], to)

    @pl.loop(1, lanes)
    def _(step):
        share_copy(lax.rem(inner + step, lanes)).start()

    share_in[inner] = shares_ref[inner]

    @pl.loop(1, lanes)
    def _(step):
        source = lax.rem(inner + step, lanes)
        remote(
            shares_ref.at[source], share_in.at[source], share_send.at[source], share_recv.at[source], source
        ).wait_recv()

    def experts_on(where):
        @pl.loop(0, 2)
        def _(turn):
            side = lax.rem(1 - core + turn, 2)
            block = rows[where, side]
            gate_part = jnp.dot(block, gate_ref[0], preferred_element_type=jnp.float32)
            up_part = jnp.dot(block, up_ref[0], preferred_element_type=jnp.float32)
            act = (gate_part / (1.0 + jnp.exp(-gate_part)) * up_part).astype(jnp.bfloat16)
            result = jnp.dot(act, down_ref[0], preferred_element_type=jnp.float32)
            share = share_in[2 * where + side]
            row_id = lax.broadcasted_iota(jnp.int32, (tok_rows, tok_rows), 0)
            col_id = lax.broadcasted_iota(jnp.int32, (tok_rows, tok_rows), 1)
            column = jnp.sum(
                jnp.where(row_id == col_id, jnp.broadcast_to(share, (tok_rows, tok_rows)), 0.0),
                axis=1, keepdims=True,
            )
            result = result.astype(jnp.bfloat16).astype(jnp.float32)
            parts[where, side] = (result * column).astype(jnp.bfloat16)

            @pl.when(turn == 0)
            def _():
                give_copy(where).start()


    def take_rows(where, onward, to):
        for k in range(CHUNKS):
            here = rows.at[where, core, at_piece(k)]
            row_copy(here, where, where, k, to).wait_recv()

            @pl.when(onward)
            def _():
                row_copy(here, where, where, k, to).start()

            mate_copy(here, where, k).start()
        for k in range(CHUNKS):
            mate_copy(rows.at[where, core, at_piece(k)], where, k).wait_recv()

    def pass_sum(where, slot_to, more, to):
        give_copy(where).wait_recv()
        for k in range(CHUNKS):
            at = at_piece(k)

            @pl.when(more)
            def _():
                sum_copy(where, where, k, to).wait_recv()
                parts[where, core, at] = (
                    parts[where, core, at].astype(jnp.float32)
                    + mate_in[where, at].astype(jnp.float32)
                    + line_in[where, at].astype(jnp.float32)
                ).astype(jnp.bfloat16)

            @pl.when(jnp.logical_not(more))
            def _():
                parts[where, core, at] = (
                    parts[where, core, at].astype(jnp.float32) + mate_in[where, at].astype(jnp.float32)
                ).astype(jnp.bfloat16)

            sum_copy(where, slot_to, k, to).start()

    for k in range(CHUNKS):
        mate_copy(rows.at[spot, core, at_piece(k)], spot, k).wait_recv()
    experts_on(spot)

    @pl.loop(1, max(2 * spots - 2, 1))
    def _(time):
        low, high = spot - time, spot + time

        @pl.when(low >= 0)
        def _():
            take_rows(low, has_above, jnp.minimum(above, lanes - 2 + core))

        @pl.when(high < spots)
        def _():
            take_rows(high, has_below, jnp.maximum(below, core))

        @pl.when(low >= 0)
        def _():
            experts_on(low)

        @pl.when(high < spots)
        def _():
            experts_on(high)

        down = 2 * spots - 2 - spot - time

        @pl.when((down >= 0) & (down < spot))
        def _():
            pass_sum(down, down, has_above, below)

        up = time - spot

        @pl.when((up > spot) & (up < spots))
        def _():
            pass_sum(up, jnp.where(up == spot + 1, spots, up), has_below, above)

    give_copy(spot).wait_recv()
    for k in range(CHUNKS):
        at = at_piece(k)
        out = parts[spot, core, at].astype(jnp.float32) + mate_in[spot, at].astype(jnp.float32)
        stash = stream[at, :] + out
        out_ref[at, :] = stash.astype(jnp.bfloat16)

        @pl.when(has_above & has_below)
        def _():
            sum_copy(spot, spot, k, above).wait_recv()
            sum_copy(spot, spots, k, above).wait_recv()
            out_ref[at, :] = (
                stash + line_in[spot, at].astype(jnp.float32) + line_in[spots, at].astype(jnp.float32)
            ).astype(jnp.bfloat16)

        @pl.when(has_above & jnp.logical_not(has_below))
        def _():
            sum_copy(spot, spot, k, above).wait_recv()
            out_ref[at, :] = (stash + line_in[spot, at].astype(jnp.float32)).astype(jnp.bfloat16)

        @pl.when(has_below & jnp.logical_not(has_above))
        def _():
            sum_copy(spot, spots, k, below).wait_recv()
            out_ref[at, :] = (stash + line_in[spots, at].astype(jnp.float32)).astype(jnp.bfloat16)

    @pl.loop(1, lanes)
    def _(step):
        share_copy(lax.rem(inner + step, lanes)).wait_send()

    for k in range(CHUNKS):
        own = rows.at[spot, core, at_piece(k)]

        @pl.when(has_above)
        def _():
            row_copy(own, spot, spot, k, above).wait_send()

        @pl.when(has_below)
        def _():
            row_copy(own, spot, spots, k, below).wait_send()

        mate_copy(own, spot, k).wait_send()

    for kind in range(2):
        for lane, (held, ahead, active) in enumerate(plan):

            @pl.when(active)
            def _():
                halo_copy(kind, held, ahead, lane).wait_send()

    @pl.loop(0, spots)
    def _(where):
        give_copy(where).wait_send()

        @pl.when(where != spot)
        def _():
            to = jnp.where(where < spot, jnp.minimum(above, lanes - 2 + core), jnp.maximum(below, core))
            back = jnp.where(where < spot, inner - 2, inner + 2)
            onward = ((where < spot) & has_above) | ((where > spot) & has_below)
            for k in range(CHUNKS):
                here = rows.at[where, core, at_piece(k)]
                mate_copy(here, where, k).wait_send()
                sum_copy(where, where, k, back).wait_send()

                @pl.when(onward)
                def _():
                    row_copy(here, where, where, k, to).wait_send()


def local(lanes, total, queries, keys, values, residual, norm_gain, w_gate, w_up, w_down, routes, gates):
    tok_rows, width = queries.shape
    spots = lanes // 2
    vmem = pl.BlockSpec(memory_space=pltpu.VMEM)
    dma = pltpu.SemaphoreType.DMA
    block = (tok_rows, width)
    return pl.pallas_call(
        functools.partial(expert_kernel, lanes, total),
        out_shape=jax.ShapeDtypeStruct(block, jnp.bfloat16),
        in_specs=[vmem] * 10,
        out_specs=vmem,
        scratch_shapes=[
            pltpu.VMEM((BACK,) + keys.shape, jnp.bfloat16),
            pltpu.VMEM((BACK,) + values.shape, jnp.bfloat16),
            pltpu.VMEM((QH, tok_rows, 1), jnp.float32),
            pltpu.VMEM((QH, tok_rows, 1), jnp.float32),
            pltpu.VMEM(block, jnp.float32),
            pltpu.VMEM((lanes, 1, tok_rows), jnp.float32),
            dma((2, 5)), dma((2, BACK)),
            pltpu.VMEM((spots, 2) + block, jnp.bfloat16),
            pltpu.VMEM((spots, 2) + block, jnp.bfloat16),
            pltpu.VMEM((spots,) + block, jnp.bfloat16),
            pltpu.VMEM((spots + 1,) + block, jnp.bfloat16),
            pltpu.VMEM((lanes, 1, tok_rows), jnp.float32),
            dma((lanes,)), dma((lanes,)),
            dma((spots + 1, CHUNKS)), dma((spots, CHUNKS)),
            dma((spots, CHUNKS)), dma((spots, CHUNKS)),
            dma((spots,)), dma((spots,)),
            dma((spots, CHUNKS)), dma((spots + 1, CHUNKS)),
        ],
        compiler_params=pltpu.CompilerParams(
            collective_id=0, has_side_effects=True, vmem_limit_bytes=60 * 1024 * 1024
        ),
    )(queries, keys, values, residual, norm_gain[None, :], routes.T, gates.T, w_gate, w_up, w_down)


def solution(mesh):
    return jax.shard_map(
        functools.partial(local, mesh.shape["inner"], mesh.shape["outer"] * mesh.shape["inner"]),
        mesh=mesh,
        in_specs=(
            P(("outer", "inner"), None),
            P(("outer", "inner"), None),
            P(("outer", "inner"), None),
            P(("outer", "inner"), None),
            P(),
            P("inner", None, None),
            P("inner", None, None),
            P("inner", None, None),
            P(("outer", "inner"), None),
            P(("outer", "inner"), None),
        ),
        out_specs=P(("outer", "inner"), None),
        check_vma=False,
    )
```

```python
import functools
import math

import jax
import jax.numpy as jnp
from jax import lax
from jax.experimental import pallas as pl
from jax.experimental.pallas import tpu as pltpu
from jax.sharding import PartitionSpec as P

D = 1024
QH = 8
KVH = 4
DH = 128
BACK = 3


MESH = pl.DeviceIdType.MESH
CHUNKS = 4
HALVES = 2


def expert_kernel(
    lanes, total, query_ref, key_ref, value_ref, residual_ref, gain_ref, route_ref, pick_ref,
    gate_ref, up_ref, down_ref, out_ref,
    key_halo, value_halo, top, mass, stream, shares_ref, halo_send, halo_recv, rows, parts, mate_in, line_in, share_in,
    share_send, share_recv, row_send, row_recv, mate_send, mate_recv,
    give_send, give_recv, sum_send, sum_recv,
):
    inner = lax.axis_index("inner")
    spots = lanes // 2
    spot, core = inner // 2, inner % 2
    mate = 2 * spot + (1 - core)
    tok_rows = query_ref.shape[0]
    groups = QH // KVH
    place = lax.axis_index("outer") * lanes + inner
    piece = tok_rows // CHUNKS
    half_rows = tok_rows // HALVES

    def at_piece(k):
        return pl.ds(pl.multiple_of(k * piece, piece), piece)

    def pieces(half):
        return [half * (CHUNKS // HALVES) + k for k in range(CHUNKS // HALVES)]

    def at_half(half):
        return pl.ds(pl.multiple_of(half * half_rows, half_rows), half_rows)

    def remote(src, dst, send, recv, to):
        return pltpu.make_async_remote_copy(
            src_ref=src, dst_ref=dst, send_sem=send, recv_sem=recv,
            device_id={"inner": to}, device_id_type=MESH,
        )

    above, below = inner + 2, inner - 2
    has_above, has_below = spot < spots - 1, spot > 0

    barrier = pltpu.get_barrier_semaphore()

    @pl.loop(1, lanes)
    def _(step):
        pl.semaphore_signal(
            barrier, inc=1, device_id={"inner": lax.rem(inner + step, lanes)}, device_id_type=MESH
        )

    def whole_id(to):
        return {"outer": to // lanes, "inner": lax.rem(to, lanes)}

    expected = lanes - 1
    for shift in (-2, -1, 1, 2):
        other = place + shift
        reaches = (other >= 0) & (other < total)

        @pl.when(reaches)
        def _():
            pl.semaphore_signal(barrier, inc=1, device_id=whole_id(other), device_id_type=MESH)

        expected = expected + reaches.astype(jnp.int32)

    @pl.loop(0, lanes)
    def _(expert):
        chosen = jnp.where(route_ref[...] == expert, pick_ref[...], 0.0)
        shares_ref[expert] = jnp.sum(chosen, axis=0, keepdims=True)

    pl.semaphore_wait(barrier, expected)

    even = core == 0
    halos = ((key_ref, key_halo), (value_ref, value_halo))

    def halo_copy(kind, held, ahead, lane):
        own_ref, halo = halos[kind]
        src = own_ref if held == 0 else halo.at[held - 1]
        return pltpu.make_async_remote_copy(
            src_ref=src, dst_ref=halo.at[held + ahead - 1],
            send_sem=halo_send.at[kind, lane], recv_sem=halo_recv.at[kind, held + ahead - 1],
            device_id=whole_id(jnp.minimum(place + ahead, total - 1)), device_id_type=MESH,
        )

    goes_one = place + 1 < total
    goes_two = even & (place + 2 < total)
    plan = (
        (0, 1, goes_one),
        (0, 2, goes_two),
        (1, 1, even & (place >= 1)),
        (1, 2, goes_two & (place >= 1)),
        (2, 1, even & (place >= 2)),
    )

    def halo_start(kind, lane):
        held, ahead, active = plan[lane]

        @pl.when(active)
        def _():
            halo_copy(kind, held, ahead, lane).start()

    def halo_wait(kind, held):
        own_ref, halo = halos[kind]

        @pl.when(place >= held)
        def _():
            pltpu.make_async_remote_copy(
                src_ref=own_ref, dst_ref=halo.at[held - 1],
                send_sem=halo_send.at[kind, 0], recv_sem=halo_recv.at[kind, held - 1],
                device_id=whole_id(jnp.maximum(place - 1, 0)), device_id_type=MESH,
            ).wait_recv()

    for lane in (1, 0):
        halo_start(0, lane)
    for lane in (1, 0):
        halo_start(1, lane)

    def attend(held):
        @pl.loop(0, KVH)
        def _(head):
            wide = pl.ds(pl.multiple_of(head * groups * DH, groups * DH), groups * DH)
            narrow = pl.ds(pl.multiple_of(head * DH, DH), DH)
            asked = query_ref[:, wide]
            if held == 0:
                keys, vals = key_ref[:, narrow], value_ref[:, narrow]
            else:
                keys, vals = key_halo[held - 1, :, narrow], value_halo[held - 1, :, narrow]
            mixed = []
            for group in range(groups):
                scores = lax.dot_general(
                    asked[:, group * DH : (group + 1) * DH], keys, (((1,), (1,)), ((), ())),
                    preferred_element_type=jnp.float32,
                ) * (1.0 / math.sqrt(DH))
                if held == 0:
                    row_id = lax.broadcasted_iota(jnp.int32, scores.shape, 0)
                    col_id = lax.broadcasted_iota(jnp.int32, scores.shape, 1)
                    scores = jnp.where(col_id <= row_id, scores, -jnp.inf)
                highest = jnp.max(scores, -1, keepdims=True)
                slot = head * groups + group
                if held:
                    highest = jnp.maximum(top[slot], highest)
                expd = jnp.exp(scores - highest)
                summed = jnp.sum(expd, -1, keepdims=True)
                part = jnp.dot(expd.astype(jnp.bfloat16), vals, preferred_element_type=jnp.float32)
                if held:
                    keep = jnp.exp(top[slot] - highest)
                    summed = summed + mass[slot] * keep
                    at = pl.ds(pl.multiple_of(slot * DH, DH), DH)
                    part = part + stream[:, at] * keep
                top[slot] = highest
                mass[slot] = summed
                mixed.append(part)
            stream[:, wide] = jnp.concatenate(mixed, 1)

    attend(0)
    for kind in range(2):
        halo_wait(kind, 1)
        halo_start(kind, 3)
        halo_start(kind, 2)
        halo_wait(kind, 2)
        halo_start(kind, 4)
    for held in range(1, BACK + 1):
        if held == BACK:
            halo_wait(0, held)
            halo_wait(1, held)

        @pl.when(place >= held)
        def _():
            attend(held)

    @pl.loop(0, QH)
    def _(slot):
        at = pl.ds(pl.multiple_of(slot * DH, DH), DH)
        attended = (stream[:, at] / mass[slot]).astype(jnp.bfloat16).astype(jnp.float32)
        stream[:, at] = residual_ref[:, at].astype(jnp.float32) + attended

    for k in range(CHUNKS):
        at = pl.ds(k * piece, piece)
        kept = stream[at, :]
        mean_sq = jnp.mean(kept * kept, -1, keepdims=True)
        rows[spot, core, at] = (kept * lax.rsqrt(mean_sq + 1e-06) * gain_ref[...]).astype(jnp.bfloat16)

    def row_copy(src, where, sem, k, to):
        return remote(src, rows.at[where, core, at_piece(k)], row_send.at[sem, k], row_recv.at[where, k], to)

    def mate_copy(src, where, k):
        return remote(src, rows.at[where, core, at_piece(k)], mate_send.at[where, k], mate_recv.at[where, k], mate)

    def give_copy(where, half):
        at = at_half(half)
        return remote(
            parts.at[where, 1 - core, at], mate_in.at[where, at],
            give_send.at[where, half], give_recv.at[where, half], mate,
        )

    def sum_copy(where, slot, k, to):
        return remote(
            parts.at[where, core, at_piece(k)], line_in.at[slot, at_piece(k)],
            sum_send.at[where, k], sum_recv.at[slot, k], to,
        )

    for k in range(CHUNKS):
        own = rows.at[spot, core, at_piece(k)]

        @pl.when(has_above)
        def _():
            row_copy(own, spot, spot, k, above).start()

        @pl.when(has_below)
        def _():
            row_copy(own, spot, spots, k, below).start()

        mate_copy(own, spot, k).start()

    def share_copy(to):
        return remote(shares_ref.at[to], share_in.at[inner], share_send.at[to], share_recv.at[inner], to)

    @pl.loop(1, lanes)
    def _(step):
        share_copy(lax.rem(inner + step, lanes)).start()

    share_in[inner] = shares_ref[inner]

    @pl.loop(1, lanes)
    def _(step):
        source = lax.rem(inner + step, lanes)
        remote(
            shares_ref.at[source], share_in.at[source], share_send.at[source], share_recv.at[source], source
        ).wait_recv()

    def experts_on(where, half):
        at = at_half(half)
        block = jnp.concatenate([rows[where, side, at] for side in range(2)], 0)
        gate_part = jnp.dot(block, gate_ref[0], preferred_element_type=jnp.float32)
        up_part = jnp.dot(block, up_ref[0], preferred_element_type=jnp.float32)
        act = (gate_part / (1.0 + jnp.exp(-gate_part)) * up_part).astype(jnp.bfloat16)
        result = jnp.dot(act, down_ref[0], preferred_element_type=jnp.float32)
        row_id = lax.broadcasted_iota(jnp.int32, (half_rows, tok_rows), 0) + half * half_rows
        col_id = lax.broadcasted_iota(jnp.int32, (half_rows, tok_rows), 1)
        for side in range(2):
            share = jnp.broadcast_to(share_in[2 * where + side], (half_rows, tok_rows))
            column = jnp.sum(jnp.where(row_id == col_id, share, 0.0), axis=1, keepdims=True)
            mine = result[side * half_rows : (side + 1) * half_rows]
            mine = mine.astype(jnp.bfloat16).astype(jnp.float32)
            parts[where, side, at] = (mine * column).astype(jnp.bfloat16)
        give_copy(where, half).start()

    def take_rows(where, half, onward, to):
        for k in pieces(half):
            here = rows.at[where, core, at_piece(k)]
            row_copy(here, where, where, k, to).wait_recv()

            @pl.when(onward)
            def _():
                row_copy(here, where, where, k, to).start()

            mate_copy(here, where, k).start()
        for k in pieces(half):
            mate_copy(rows.at[where, core, at_piece(k)], where, k).wait_recv()

    def pass_sum(where, half, slot_to, more, to):
        give_copy(where, half).wait_recv()
        for k in pieces(half):
            at = at_piece(k)

            @pl.when(more)
            def _():
                sum_copy(where, where, k, to).wait_recv()
                parts[where, core, at] = (
                    parts[where, core, at].astype(jnp.float32)
                    + mate_in[where, at].astype(jnp.float32)
                    + line_in[where, at].astype(jnp.float32)
                ).astype(jnp.bfloat16)

            @pl.when(jnp.logical_not(more))
            def _():
                parts[where, core, at] = (
                    parts[where, core, at].astype(jnp.float32) + mate_in[where, at].astype(jnp.float32)
                ).astype(jnp.bfloat16)

            sum_copy(where, slot_to, k, to).start()

    @pl.loop(0, HALVES)
    def _(half):
        for k in pieces(half):
            mate_copy(rows.at[spot, core, at_piece(k)], spot, k).wait_recv()
        experts_on(spot, half)

    @pl.loop(HALVES, max(2 * spots - 2, 1) * HALVES)
    def _(tick):
        time, half = tick // HALVES, lax.rem(tick, HALVES)
        low, high = spot - time, spot + time

        @pl.when(low >= 0)
        def _():
            take_rows(low, half, has_above, jnp.minimum(above, lanes - 2 + core))

        @pl.when(high < spots)
        def _():
            take_rows(high, half, has_below, jnp.maximum(below, core))

        @pl.when(low >= 0)
        def _():
            experts_on(low, half)

        @pl.when(high < spots)
        def _():
            experts_on(high, half)

        down = 2 * spots - 2 - spot - time

        @pl.when((down >= 0) & (down < spot))
        def _():
            pass_sum(down, half, down, has_above, below)

        up = time - spot

        @pl.when((up > spot) & (up < spots))
        def _():
            pass_sum(up, half, jnp.where(up == spot + 1, spots, up), has_below, above)

    for half in range(HALVES):
        give_copy(spot, half).wait_recv()
    for k in range(CHUNKS):
        at = at_piece(k)
        out = parts[spot, core, at].astype(jnp.float32) + mate_in[spot, at].astype(jnp.float32)
        stash = stream[at, :] + out
        out_ref[at, :] = stash.astype(jnp.bfloat16)

        @pl.when(has_above & has_below)
        def _():
            sum_copy(spot, spot, k, above).wait_recv()
            sum_copy(spot, spots, k, above).wait_recv()
            out_ref[at, :] = (
                stash + line_in[spot, at].astype(jnp.float32) + line_in[spots, at].astype(jnp.float32)
            ).astype(jnp.bfloat16)

        @pl.when(has_above & jnp.logical_not(has_below))
        def _():
            sum_copy(spot, spot, k, above).wait_recv()
            out_ref[at, :] = (stash + line_in[spot, at].astype(jnp.float32)).astype(jnp.bfloat16)

        @pl.when(has_below & jnp.logical_not(has_above))
        def _():
            sum_copy(spot, spots, k, below).wait_recv()
            out_ref[at, :] = (stash + line_in[spots, at].astype(jnp.float32)).astype(jnp.bfloat16)

    @pl.loop(1, lanes)
    def _(step):
        share_copy(lax.rem(inner + step, lanes)).wait_send()

    for k in range(CHUNKS):
        own = rows.at[spot, core, at_piece(k)]

        @pl.when(has_above)
        def _():
            row_copy(own, spot, spot, k, above).wait_send()

        @pl.when(has_below)
        def _():
            row_copy(own, spot, spots, k, below).wait_send()

        mate_copy(own, spot, k).wait_send()

    for kind in range(2):
        for lane, (held, ahead, active) in enumerate(plan):

            @pl.when(active)
            def _():
                halo_copy(kind, held, ahead, lane).wait_send()

    @pl.loop(0, spots)
    def _(where):
        for half in range(HALVES):
            give_copy(where, half).wait_send()

        @pl.when(where != spot)
        def _():
            to = jnp.where(where < spot, jnp.minimum(above, lanes - 2 + core), jnp.maximum(below, core))
            back = jnp.where(where < spot, inner - 2, inner + 2)
            onward = ((where < spot) & has_above) | ((where > spot) & has_below)
            for k in range(CHUNKS):
                here = rows.at[where, core, at_piece(k)]
                mate_copy(here, where, k).wait_send()
                sum_copy(where, where, k, back).wait_send()

                @pl.when(onward)
                def _():
                    row_copy(here, where, where, k, to).wait_send()


def local(lanes, total, queries, keys, values, residual, norm_gain, w_gate, w_up, w_down, routes, gates):
    tok_rows, width = queries.shape
    spots = lanes // 2
    vmem = pl.BlockSpec(memory_space=pltpu.VMEM)
    dma = pltpu.SemaphoreType.DMA
    block = (tok_rows, width)
    return pl.pallas_call(
        functools.partial(expert_kernel, lanes, total),
        out_shape=jax.ShapeDtypeStruct(block, jnp.bfloat16),
        in_specs=[vmem] * 10,
        out_specs=vmem,
        scratch_shapes=[
            pltpu.VMEM((BACK,) + keys.shape, jnp.bfloat16),
            pltpu.VMEM((BACK,) + values.shape, jnp.bfloat16),
            pltpu.VMEM((QH, tok_rows, 1), jnp.float32),
            pltpu.VMEM((QH, tok_rows, 1), jnp.float32),
            pltpu.VMEM(block, jnp.float32),
            pltpu.VMEM((lanes, 1, tok_rows), jnp.float32),
            dma((2, 5)), dma((2, BACK)),
            pltpu.VMEM((spots, 2) + block, jnp.bfloat16),
            pltpu.VMEM((spots, 2) + block, jnp.bfloat16),
            pltpu.VMEM((spots,) + block, jnp.bfloat16),
            pltpu.VMEM((spots + 1,) + block, jnp.bfloat16),
            pltpu.VMEM((lanes, 1, tok_rows), jnp.float32),
            dma((lanes,)), dma((lanes,)),
            dma((spots + 1, CHUNKS)), dma((spots, CHUNKS)),
            dma((spots, CHUNKS)), dma((spots, CHUNKS)),
            dma((spots, HALVES)), dma((spots, HALVES)),
            dma((spots, CHUNKS)), dma((spots + 1, CHUNKS)),
        ],
        compiler_params=pltpu.CompilerParams(
            collective_id=0, has_side_effects=True, vmem_limit_bytes=60 * 1024 * 1024
        ),
    )(queries, keys, values, residual, norm_gain[None, :], routes.T, gates.T, w_gate, w_up, w_down)


def solution(mesh):
    return jax.shard_map(
        functools.partial(local, mesh.shape["inner"], mesh.shape["outer"] * mesh.shape["inner"]),
        mesh=mesh,
        in_specs=(
            P(("outer", "inner"), None),
            P(("outer", "inner"), None),
            P(("outer", "inner"), None),
            P(("outer", "inner"), None),
            P(),
            P("inner", None, None),
            P("inner", None, None),
            P("inner", None, None),
            P(("outer", "inner"), None),
            P(("outer", "inner"), None),
        ),
        out_specs=P(("outer", "inner"), None),
        check_vma=False,
    )
```
